32 devices in a mesh: users: 8 (over y, x, core), hist: 4 (over z).
Axes of the slice: x: 2, y: 2, z: 4, core: 2. Of those that a mesh axis runs over, the one named last changes fastest.
Arguments:
- cand_x: bfloat16 [2048, 512], P(('users', 'hist')), parts along dimension 0, may hold values from -6 to 6
- hist_keys: bfloat16 [16384, 512], P(('users', 'hist')), parts along dimension 0, may hold values from -6 to 6
- hist_values: bfloat16 [16384, 512], P(('users', 'hist')), parts along dimension 0, may hold values from -6 to 6
- key_scale: bfloat16 [16384], P(('users', 'hist')), parts along dimension 0, may hold values from 0.5 to 2
- hist_len: int32 [8], P('users'), parts along dimension 0, may hold values from 512 to 2048
- cand_limit: int32 [2048], P('users'), parts along dimension 0, may hold values from 1 to 2048
- ln_gain: float32 [512], replicated, may hold values from 0.1 to 1.9
- w_qu: bfloat16 [512, 1024], replicated, may hold values from -0.25 to 0.25
- w_out: bfloat16 [512, 512], replicated, may hold values from -0.25 to 0.25
Outputs:
- scored: bfloat16 [2048, 512], P(('users', 'hist')), parts along dimension 0
The draws below stay inside these ranges and needn't reach their ends.
There are 8 independent parts, one for each index of `users`. The reference program is written for one: setup_inputs(seed, part) draws one part's arguments, and reference() takes and returns one part's arrays. A program takes and returns all parts, laid end to end along the dimension named above; an argument that names none is the same for every part. Nothing has to cross between parts.
All inputs are finite; a program needn't handle non-finite values.
Results may differ from the reference program's by a relative error of at most 0.0058.
Values may be sent and summed in bfloat16 or wider, within the bound.
A program may use at most 64 MiB of HBM per device.

```python
import math
import jax
import jax.numpy as jnp
from jax import lax

D = 512
HEADS = 8
CAND_DEV = 64
NC = 256
HIST = 2048


def touch_ends(result, stream_key, low, largest):
    shape = result.shape
    index_at = [jax.random.randint(jax.random.fold_in(stream_key, axis), (), 0, shape[axis]) for axis in range(len(shape))]
    result = result.at[tuple(index_at)].set(low)
    longest = shape.index(max(shape))
    index_at[longest] = (index_at[longest] + 1) % shape[longest]
    return result.at[tuple(index_at)].set(largest)


def levels(rng, shape, pieces, smallest, top_value):
    factor_of = 1.0
    for position, shards_of in pieces:
        heights = jax.random.uniform(jax.random.fold_in(jax.random.fold_in(rng, 6), position), (shards_of,), jnp.float32, smallest / len(pieces), top_value / len(pieces))
        factor_of = factor_of * jnp.repeat(jnp.exp(heights), shape[position] // shards_of).reshape((-1,) + (1,) * (len(shape) - 1 - position))
    return factor_of


def noise(rng, extent, deviation, reach, pieces=(), held_as=jnp.bfloat16):
    level = levels(rng, extent, pieces, -0.22, 0.18) if pieces else 1.0
    array = jax.random.normal(rng, extent, jnp.float32) * deviation * level
    return jnp.minimum(jnp.maximum(array, -reach), reach).astype(held_as)


def setup_inputs(seed: int = 0, part: int = 0) -> dict:
    arg_keys = jax.random.split(jax.random.key(seed), 10)
    part_splits = jax.random.split(jax.random.fold_in(arg_keys[9], part), 10)
    cand_x = noise(part_splits[0], (NC, D), 1.0, 6.0, ((0, 4),))
    hist_keys = noise(part_splits[1], (HIST, D), 1.0, 6.0, ((0, 4),))
    hist_values = noise(part_splits[2], (HIST, D), 1.0, 6.0, ((0, 4),))
    key_scale = jnp.clip(jnp.exp(math.log(2.0) - 1.3862944 * jax.random.uniform(part_splits[3], (HIST,), jnp.float32) ** levels(part_splits[3], (HIST,), ((0, 4),), -0.2, 0.2)), 0.5, 2.0).astype(jnp.bfloat16)
    hist_len = jax.random.randint(part_splits[4], (1,), HIST // 4, HIST + 1).astype(jnp.int32)
    cand_limit = touch_ends(jax.random.randint(part_splits[5], (NC,), 1, HIST + 1), jax.random.fold_in(part_splits[5], 1), 1, HIST).astype(jnp.int32)
    ln_gain = jnp.clip(1.0 + 0.18 * jax.random.normal(arg_keys[6], (D,), jnp.float32), 0.1, 1.9)
    w_qu = noise(arg_keys[7], (D, 2 * D), D ** -0.5, 0.25)
    w_out = noise(arg_keys[8], (D, D), D ** -0.5, 0.25)
    return dict(cand_x=cand_x, hist_keys=hist_keys, hist_values=hist_values, key_scale=key_scale, hist_len=hist_len, cand_limit=cand_limit, ln_gain=ln_gain, w_qu=w_qu, w_out=w_out)


def row_norm(values):
    center = lax.optimization_barrier(jnp.mean(values, axis=-1, keepdims=True))
    spread = lax.optimization_barrier(jnp.mean((values - center) ** 2, axis=-1, keepdims=True))
    return (values - center) / jnp.sqrt(spread + 1e-05)

def attend(query_rows, history_limits, key_rows, value_rows, scale_rows, offset_pos):
    count = query_rows.shape[0]
    length = key_rows.shape[0]
    width = query_rows.shape[1]
    head_size = width // HEADS
    query_head_blocks = query_rows.reshape(count, HEADS, head_size)
    key_head_blocks = key_rows.reshape(length, HEADS, head_size)
    value_head_blocks = value_rows.reshape(length, HEADS, head_size)
    attention_scores = jnp.einsum('ufe,yfe->fuy', query_head_blocks, key_head_blocks, preferred_element_type=jnp.float32)
    factor = scale_rows.astype(jnp.float32) / jnp.sqrt(jnp.float32(head_size))
    attention_scores = attention_scores * factor[None, None, :]
    positions = offset_pos + jnp.arange(length, dtype=jnp.int32)
    visible = positions[None, :] < history_limits[:, None]
    weight_matrices = jnp.where(visible[None], jax.nn.silu(attention_scores), 0.0).astype(jnp.bfloat16)
    summed_output = jnp.einsum('apn,naf->paf', weight_matrices, value_head_blocks, preferred_element_type=jnp.float32)
    return summed_output.reshape(count, width)

def reference(cand_x, hist_keys, hist_values, key_scale, hist_len, cand_limit, ln_gain, w_qu, w_out):
    inputs32 = cand_x.astype(jnp.float32)
    normed = (row_norm(inputs32) * ln_gain).astype(jnp.bfloat16)
    projected = jax.nn.silu(jnp.dot(normed, w_qu, preferred_element_type=jnp.float32))
    query_vectors = projected[:, :D].astype(jnp.bfloat16)
    gating = projected[:, D:]
    history_limits = jnp.minimum(cand_limit, hist_len[0]).astype(jnp.int32)
    blocks = NC // CAND_DEV

    def one_block(couple):
        return attend(couple[0], couple[1], hist_keys, hist_values, key_scale, jnp.int32(0))
    attended = lax.map(one_block, (query_vectors.reshape(blocks, CAND_DEV, D), history_limits.reshape(blocks, CAND_DEV)))
    attended = attended.reshape(NC, D)
    mixed = (row_norm(attended) * gating).astype(jnp.bfloat16)
    return (inputs32 + jnp.dot(mixed, w_out, preferred_element_type=jnp.float32)).astype(jnp.bfloat16)
```

```python
import functools

import jax
import jax.numpy as jnp
from jax import lax
from jax.experimental import pallas as pl
from jax.experimental.pallas import tpu as pltpu
from jax.sharding import PartitionSpec as P

HEADS = 8
GROUP = 4
LANES = 128
MESH = pl.DeviceIdType.MESH


def partner_of(me, step, count):
    bit = 1
    partner = me
    while bit < count:
        if step & bit:
            partner = partner + bit * (1 - 2 * lax.rem(me // bit, 2))
        bit *= 2
    return partner


def half_silu(half):
    return half + half * jnp.tanh(half)


def row_norm(values):
    center = jnp.mean(values, axis=-1, keepdims=True)
    spread = jnp.mean((values - center) ** 2, axis=-1, keepdims=True)
    return (values - center) / jnp.sqrt(spread + 1e-05)


def kernel(
    count,
    x_hbm, keys_hbm, values_hbm, scale_hbm, len_hbm, limit_hbm, gain_hbm, wqu_hbm, wout_hbm,
    out_ref,
    x_buf, keys_buf, values_buf, scale_buf, len_buf, limit_buf, gain_buf, wqu_buf, wout_buf,
    keys_t, limit_col, got_x, send_sum, got_sum,
    local_sem, xs_sem, xr_sem, ss_sem, sr_sem,
):
    me = lax.axis_index("hist")
    rows, width = x_buf.shape
    length = keys_buf.shape[0]
    head = width // HEADS
    span = GROUP * head
    steps = sorted(range(1, count), key=lambda step: -step)

    barrier = pltpu.get_barrier_semaphore()
    for step in steps:
        pl.semaphore_signal(
            barrier, inc=1, device_id={"hist": partner_of(me, step, count)}, device_id_type=MESH
        )

    pairs = [
        (x_hbm, x_buf), (limit_hbm, limit_buf), (len_hbm, len_buf), (gain_hbm, gain_buf),
        (scale_hbm, scale_buf), (keys_hbm, keys_buf), (wqu_hbm, wqu_buf),
        (values_hbm, values_buf), (wout_hbm, wout_buf),
    ]
    loads = [
        pltpu.make_async_copy(src, dst, local_sem.at[i]) for i, (src, dst) in enumerate(pairs)
    ]
    for load in loads:
        load.start()
    x_in, limit_in, len_in, gain_in, scale_in, keys_in, wqu_in, values_in, wout_in = loads
    x_in.wait()
    limit_in.wait()
    len_in.wait()
    limits = jnp.minimum(limit_buf[...], len_buf[0]).astype(jnp.float32).reshape(1, -1)
    limit_col[...] = jnp.broadcast_to(limits, (LANES, limits.shape[1])).T

    pl.semaphore_wait(barrier, count - 1)
    x_copies = {}
    for step in steps:
        x_copies[step] = pltpu.make_async_remote_copy(
            src_ref=x_buf,
            dst_ref=got_x.at[step - 1],
            send_sem=xs_sem.at[step - 1],
            recv_sem=xr_sem.at[step - 1],
            device_id={"hist": partner_of(me, step, count)},
            device_id_type=MESH,
        )
        x_copies[step].start()

    gain_in.wait()
    scale_in.wait()
    keys_in.wait()
    keys_t[...] = keys_buf[...].T
    gain = gain_buf[...].reshape(1, width)
    factor_row = scale_buf[...].astype(jnp.float32).reshape(1, length) * (0.5 / head**0.5)
    positions = (
        lax.broadcasted_iota(jnp.int32, (rows, length), 1) + me * length
    ).astype(jnp.float32)
    head_of_lane = lax.broadcasted_iota(jnp.int32, (rows, span), 1) // head

    def normed_of(block):
        return (row_norm(block.astype(jnp.float32)) * gain).astype(jnp.bfloat16)

    def attend(normed, owner):
        raw = jnp.dot(normed, wqu_buf[:, :width], preferred_element_type=jnp.float32)
        queries = half_silu(raw * 0.5)
        own_limit = limit_col[pl.ds(pl.multiple_of(owner * rows, rows), rows), :]
        own_limit = jnp.concatenate([own_limit] * (length // LANES), axis=1)
        factor = jnp.where(positions < own_limit, factor_row, 0.0)
        factor = jnp.concatenate([factor] * GROUP, axis=0)
        parts = []
        for start in range(0, width, span):
            some = queries[:, start : start + span]
            stacked = jnp.concatenate(
                [jnp.where(head_of_lane == i, some, 0.0) for i in range(GROUP)], axis=0
            ).astype(jnp.bfloat16)
            scores = jnp.dot(
                stacked, keys_t[start : start + span, :], preferred_element_type=jnp.float32
            )
            weights = half_silu(scores * factor).astype(jnp.bfloat16)
            summed = jnp.dot(
                weights, values_buf[:, start : start + span], preferred_element_type=jnp.float32
            )
            part = summed[:rows]
            for i in range(1, GROUP):
                part = jnp.where(head_of_lane == i, summed[i * rows : (i + 1) * rows], part)
            parts.append(part)
        return jnp.concatenate(parts, axis=1)

    normed = normed_of(x_buf[...])
    wqu_in.wait()
    values_in.wait()
    total = attend(normed, me)
    gating = half_silu(
        0.5 * jnp.dot(normed, wqu_buf[:, width:], preferred_element_type=jnp.float32)
    )

    sum_copies = {}
    for step in steps:
        partner = partner_of(me, step, count)
        x_copies[step].wait_recv()
        send_sum[step - 1] = attend(normed_of(got_x[step - 1]), partner).astype(jnp.bfloat16)
        sum_copies[step] = pltpu.make_async_remote_copy(
            src_ref=send_sum.at[step - 1],
            dst_ref=got_sum.at[step - 1],
            send_sem=ss_sem.at[step - 1],
            recv_sem=sr_sem.at[step - 1],
            device_id={"hist": partner},
            device_id_type=MESH,
        )
        sum_copies[step].start()

    wout_in.wait()
    for step in steps:
        sum_copies[step].wait_recv()
        total = total + got_sum[step - 1].astype(jnp.float32)
    mixed = (row_norm(total) * gating).astype(jnp.bfloat16)
    scored = x_buf[...].astype(jnp.float32) + jnp.dot(
        mixed, wout_buf[...], preferred_element_type=jnp.float32
    )
    out_ref[...] = scored.astype(jnp.bfloat16)
    for step in steps:
        x_copies[step].wait_send()
        sum_copies[step].wait_send()


def on_device(*args):
    count = lax.axis_size("hist")
    cand_x, limit = args[0], args[5]
    rows, width = cand_x.shape
    length = args[1].shape[0]
    assert count & (count - 1) == 0
    peers = count - 1
    block = (peers, rows, width)
    scratch = [
        pltpu.SMEM(a.shape, a.dtype) if i == 4 else pltpu.VMEM(a.shape, a.dtype)
        for i, a in enumerate(args)
    ]
    scratch += [
        pltpu.VMEM((width, length), jnp.bfloat16),
        pltpu.VMEM((limit.shape[0], LANES), jnp.float32),
        pltpu.VMEM(block, jnp.bfloat16),
        pltpu.VMEM(block, jnp.bfloat16),
        pltpu.VMEM(block, jnp.bfloat16),
        pltpu.SemaphoreType.DMA((len(args),)),
    ]
    scratch += [pltpu.SemaphoreType.DMA((peers,))] * 4
    return pl.pallas_call(
        functools.partial(kernel, count),
        out_shape=jax.ShapeDtypeStruct((rows, width), jnp.bfloat16),
        in_specs=[pl.BlockSpec(memory_space=pl.ANY)] * len(args),
        out_specs=pl.BlockSpec(memory_space=pltpu.VMEM),
        scratch_shapes=scratch,
        compiler_params=pltpu.CompilerParams(
            collective_id=0, has_side_effects=True, vmem_limit_bytes=60 * 1024 * 1024
        ),
    )(*args)


def solution(mesh):
    both = ("users", "hist")
    in_specs = (
        P(both, None), P(both, None), P(both, None), P(both), P("users"), P("users"),
        P(), P(), P(),
    )
    return jax.shard_map(
        on_device, mesh=mesh, in_specs=in_specs, out_specs=P(both, None), check_vma=False
    )
```

```python
import functools

import jax
import jax.numpy as jnp
from jax import lax
from jax.experimental import pallas as pl
from jax.experimental.pallas import tpu as pltpu
from jax.sharding import PartitionSpec as P

HEADS = 8
GROUP = 4
LANES = 128
PIECES = 2
MESH = pl.DeviceIdType.MESH


def partner_of(me, step, count):
    bit = 1
    partner = me
    while bit < count:
        if step & bit:
            partner = partner + bit * (1 - 2 * lax.rem(me // bit, 2))
        bit *= 2
    return partner


def half_silu(half):
    return half + half * jnp.tanh(half)


def row_norm(values):
    center = jnp.mean(values, axis=-1, keepdims=True)
    spread = jnp.mean((values - center) ** 2, axis=-1, keepdims=True)
    return (values - center) / jnp.sqrt(spread + 1e-05)


def kernel(
    count,
    x_hbm, keys_hbm, values_hbm, scale_hbm, len_hbm, limit_hbm, gain_hbm, wqu_hbm, wout_hbm,
    out_ref,
    x_buf, keys_buf, values_buf, scale_buf, len_buf, limit_buf, gain_buf, wqu_buf, wout_buf,
    keys_t, limit_col, got_x, send_sum, got_sum,
    local_sem, xs_sem, xr_sem, ss_sem, sr_sem,
):
    me = lax.axis_index("hist")
    rows, width = x_buf.shape
    length = keys_buf.shape[0]
    head = width // HEADS
    span = GROUP * head
    half = count // 2
    near = range(1, half)

    def to(step):
        return {"hist": partner_of(me, step, count)}

    def pieces(step):
        size = rows if step in near else rows // PIECES
        return [(i, pl.ds(i * size, size)) for i in range(rows // size)]

    barrier = pltpu.get_barrier_semaphore()
    for step in range(1, half + 1):
        pl.semaphore_signal(barrier, inc=1, device_id=to(step), device_id_type=MESH)

    pairs = [
        (x_hbm, x_buf), (limit_hbm, limit_buf), (len_hbm, len_buf), (gain_hbm, gain_buf),
        (scale_hbm, scale_buf), (keys_hbm, keys_buf), (wqu_hbm, wqu_buf),
        (values_hbm, values_buf), (wout_hbm, wout_buf),
    ]
    loads = [
        pltpu.make_async_copy(src, dst, local_sem.at[i]) for i, (src, dst) in enumerate(pairs)
    ]
    for load in loads:
        load.start()
    x_in, limit_in, len_in, gain_in, scale_in, keys_in, wqu_in, values_in, wout_in = loads
    pl.semaphore_wait(barrier, half)
    sends = []

    def send(source, target, send_sem, recv_sem, step):
        copy = pltpu.make_async_remote_copy(
            src_ref=source, dst_ref=target, send_sem=send_sem, recv_sem=recv_sem,
            device_id=to(step), device_id_type=MESH,
        )
        copy.start()
        sends.append(copy)

    def send_x(source, step, i, part, hop):
        send(source, got_x.at[step - 1, part], xs_sem.at[step - 1, i], xr_sem.at[step - 1, i], hop)

    def wait_block(buffer, sem, step, i, part):
        block = buffer.at[step - 1, part]
        pltpu.make_async_remote_copy(
            src_ref=block, dst_ref=block, send_sem=sem.at[step - 1, i],
            recv_sem=sem.at[step - 1, i], device_id=to(step), device_id_type=MESH,
        ).wait_recv()

    for step in [half, *near]:
        for i, part in pieces(step):
            send_x(x_hbm.at[part], step, i, part, step)

    x_in.wait()
    limit_in.wait()
    len_in.wait()
    limits = jnp.minimum(
        limit_buf[...].reshape(1, -1), len_buf[...].reshape(1, 1)
    ).astype(jnp.float32)
    limit_col[...] = jnp.broadcast_to(limits, (LANES, limits.shape[1])).T
    gain_in.wait()
    scale_in.wait()
    keys_in.wait()
    keys_t[...] = keys_buf[...].T
    gain = gain_buf[...].reshape(1, width)
    factor_row = scale_buf[...].astype(jnp.float32).reshape(1, length) * (0.5 / head**0.5)
    positions = (
        lax.broadcasted_iota(jnp.int32, (rows, length), 1) + me * length
    ).astype(jnp.float32)
    head_of_lane = lax.broadcasted_iota(jnp.int32, (rows, span), 1) // head

    def normed_of(block):
        return (row_norm(block.astype(jnp.float32)) * gain).astype(jnp.bfloat16)

    def attend(normed, first):
        rows = normed.shape[0]
        lane_head = head_of_lane[:rows]
        raw = jnp.dot(normed, wqu_buf[:, :width], preferred_element_type=jnp.float32)
        queries = half_silu(raw * 0.5)
        own_limit = limit_col[pl.ds(pl.multiple_of(first, rows), rows), :]
        own_limit = jnp.concatenate([own_limit] * (length // LANES), axis=1)
        factor = jnp.where(positions[:rows] < own_limit, factor_row, 0.0)
        factor = jnp.concatenate([factor] * GROUP, axis=0)
        parts = []
        for start in range(0, width, span):
            some = queries[:, start : start + span]
            stacked = jnp.concatenate(
                [jnp.where(lane_head == i, some, 0.0) for i in range(GROUP)], axis=0
            ).astype(jnp.bfloat16)
            scores = jnp.dot(
                stacked, keys_t[start : start + span, :], preferred_element_type=jnp.float32
            )
            weights = half_silu(scores * factor).astype(jnp.bfloat16)
            summed = jnp.dot(
                weights, values_buf[:, start : start + span], preferred_element_type=jnp.float32
            )
            part = summed[:rows]
            for i in range(1, GROUP):
                part = jnp.where(lane_head == i, summed[i * rows : (i + 1) * rows], part)
            parts.append(part)
        return jnp.concatenate(parts, axis=1)

    normed = normed_of(x_buf[...])
    wqu_in.wait()
    values_in.wait()
    total = attend(normed, me * rows)
    gating = half_silu(
        0.5 * jnp.dot(normed, wqu_buf[:, width:], preferred_element_type=jnp.float32)
    )

    def answer(step, i, part):
        first = partner_of(me, step, count) * rows + part.start
        send_sum[step - 1, part] = attend(normed_of(got_x[step - 1, part]), first).astype(
            jnp.bfloat16
        )
        send(
            send_sum.at[step - 1, part], got_sum.at[step - 1, part],
            ss_sem.at[step - 1, i], sr_sem.at[step - 1, i], step,
        )

    for i, part in pieces(half):
        wait_block(got_x, xr_sem, half, i, part)
        for step in near:
            send_x(got_x.at[half - 1, part], half + step, i, part, step)
        answer(half, i, part)
    for step in near:
        for i, part in pieces(step):
            wait_block(got_x, xr_sem, step, i, part)
            answer(step, i, part)
    for i in range(PIECES):
        for step in range(half + 1, count):
            part = pieces(step)[i][1]
            wait_block(got_x, xr_sem, step, i, part)
            answer(step, i, part)

    wout_in.wait()
    for step in [*near, *range(half, count)]:
        for i, part in pieces(step):
            wait_block(got_sum, sr_sem, step, i, part)
        total = total + got_sum[step - 1].astype(jnp.float32)
    mixed = (row_norm(total) * gating).astype(jnp.bfloat16)
    scored = x_buf[...].astype(jnp.float32) + jnp.dot(
        mixed, wout_buf[...], preferred_element_type=jnp.float32
    )
    out_ref[...] = scored.astype(jnp.bfloat16)
    for copy in sends:
        copy.wait_send()


def on_device(*args):
    count = lax.axis_size("hist")
    cand_x, limit = args[0], args[5]
    rows, width = cand_x.shape
    length = args[1].shape[0]
    assert count & (count - 1) == 0
    peers = count - 1
    block = (peers, rows, width)
    scratch = [
        pltpu.VMEM(a.shape, a.dtype) for a in args
    ]
    scratch += [
        pltpu.VMEM((width, length), jnp.bfloat16),
        pltpu.VMEM((limit.shape[0], LANES), jnp.float32),
        pltpu.VMEM(block, jnp.bfloat16),
        pltpu.VMEM(block, jnp.bfloat16),
        pltpu.VMEM(block, jnp.bfloat16),
        pltpu.SemaphoreType.DMA((len(args),)),
    ]
    scratch += [pltpu.SemaphoreType.DMA((peers, PIECES))] * 4
    return pl.pallas_call(
        functools.partial(kernel, count),
        out_shape=jax.ShapeDtypeStruct((rows, width), jnp.bfloat16),
        in_specs=[pl.BlockSpec(memory_space=pl.ANY)] * len(args),
        out_specs=pl.BlockSpec(memory_space=pltpu.VMEM),
        scratch_shapes=scratch,
        compiler_params=pltpu.CompilerParams(
            collective_id=0, has_side_effects=True, vmem_limit_bytes=60 * 1024 * 1024
        ),
    )(*args)


def solution(mesh):
    both = ("users", "hist")
    in_specs = (
        P(both, None), P(both, None), P(both, None), P(both), P("users"), P("users"),
        P(), P(), P(),
    )
    return jax.shard_map(
        on_device, mesh=mesh, in_specs=in_specs, out_specs=P(both, None), check_vma=False
    )
```
